32 devices in a mesh: fsdp: 8 (over y, x, core), dp: 4 (over z).
Axes of the slice: x: 2, y: 2, z: 4, core: 2. Of those that a mesh axis runs over, the one named last changes fastest.
Arguments:
- hidden: bfloat16 [8192, 14336], P(('fsdp', 'dp')), may hold values from -6 to 6
- cotangent: bfloat16 [8192, 4096], P(('fsdp', 'dp')), may hold values from -6 to 6
- tiles: bfloat16 [64, 128, 128], P('fsdp'), may hold values from -0.25 to 0.25
- tile_rows: int32 [64], P('fsdp'), may hold values from 0 to 111, as said below
- tile_cols: int32 [64], P('fsdp'), may hold values from 0 to 31, as said below
- counts: int32 [8], P('fsdp'), may hold values from 1 to 8, as said below
Outputs:
- layer_out: bfloat16 [8192, 4096], P(('fsdp', 'dp'))
- hidden_grad: bfloat16 [8192, 14336], P(('fsdp', 'dp'))
- weight_grad: float32 [64, 128, 128], P('fsdp')
The draws below stay inside these ranges and needn't reach their ends.
Inputs may be any that keep to these rules, and one draw needn't show every extreme that they name: `tile_rows`: every slot (live or not) names a different block; the row block is below 112. `tile_cols`: the column block is below 32. `counts`: some owner has all 8 slots live in every draw.
All inputs are finite; a program needn't handle non-finite values.
Results may differ from the reference program's by a relative error of at most 0.0085.
Values may be sent and summed in bfloat16 or wider, within the bound.
A program may use at most 192 MiB of HBM per device.

```python
import math
import jax
import jax.numpy as jnp
from jax import lax

D = 4096
FF = 14336
TILE = 128
MAXB = 8
SLOTS = 64
TOKENS = 8192
N_FSDP = 8


def chosen_blocks(key):
    ordering = jax.random.permutation(jax.random.fold_in(key, 11), FF // TILE * (D // TILE))
    picked = ordering[:SLOTS].astype(jnp.int32)
    return jnp.sort(picked).astype(jnp.int32)


def draw_tile_rows(key, part):
    return (chosen_blocks(key) // (D // TILE)).astype(jnp.int32)


def draw_tile_cols(key, part):
    return (chosen_blocks(key) % (D // TILE)).astype(jnp.int32)


def draw_counts(key, part):
    drawn = jax.random.randint(jax.random.fold_in(key, 3), (N_FSDP,), 1, MAXB + 1)
    fullest = jax.random.randint(jax.random.fold_in(key, 5), (), 0, N_FSDP)
    return jnp.where(jnp.arange(N_FSDP) == fullest, MAXB, drawn).astype(jnp.int32)


def draw_hidden(key, part):
    own_key = jax.random.fold_in(key, 21)
    rough_key = jax.random.fold_in(key, 22)
    position = jnp.arange(FF, dtype=jnp.float32) / TILE
    level = jnp.floor(position) / max(FF // TILE - 1, 1)
    rough = jax.random.uniform(rough_key, (FF,), jnp.float32, 0.8, 1.25)
    column_scale = 0.6 * jnp.exp(level * jnp.log(2.0 / 0.6)) * rough
    values = jax.random.truncated_normal(own_key, -2.4, 2.4, (TOKENS, FF), jnp.float32) * column_scale[None, :]
    return values.astype(jnp.bfloat16)


def draw_cotangent(key, part):
    own_key = jax.random.fold_in(key, 23)
    values = jax.random.truncated_normal(own_key, -6.0, 6.0, (TOKENS, D), jnp.float32)
    return values.astype(jnp.bfloat16)


def block_scale(key, dims, cuts, low, high):
    level = 1.0
    for dim, shards_of in cuts:
        draws = jax.random.uniform(jax.random.fold_in(jax.random.fold_in(key, 6), dim), (shards_of,), jnp.float32, low / len(cuts), high / len(cuts))
        level = level * jnp.repeat(jnp.exp(draws), dims[dim] // shards_of).reshape((-1,) + (1,) * (len(dims) - 1 - dim))
    return level


def bell_draw(stream_key, dims, scale, limit, cuts=(), held_as=jnp.bfloat16):
    gain = block_scale(stream_key, dims, cuts, -0.22, 0.18) if cuts else 1.0
    array = jax.random.normal(stream_key, dims, jnp.float32) * scale * gain
    return jnp.minimum(jnp.maximum(array, -limit), limit).astype(held_as)


def setup_inputs(seed: int = 0) -> dict:
    arg_keys = jax.random.split(jax.random.key(seed), 7)
    return {
        "hidden": draw_hidden(jax.random.fold_in(arg_keys[6], 71), 0),
        "cotangent": draw_cotangent(jax.random.fold_in(arg_keys[6], 71), 0),
        "tiles": bell_draw(arg_keys[2], (SLOTS, TILE, TILE), (TILE * MAXB // 2) ** -0.5, 0.25, ((0, 8),)),
        "tile_rows": draw_tile_rows(jax.random.fold_in(arg_keys[6], 71), 0),
        "tile_cols": draw_tile_cols(jax.random.fold_in(arg_keys[6], 71), 0),
        "counts": draw_counts(jax.random.fold_in(arg_keys[6], 71), 0),
    }


def reference(hidden, cotangent, tiles, tile_rows, tile_cols, counts):
    slot_total = tiles.shape[0]
    per_owner = slot_total // N_FSDP
    edge_len = tiles.shape[1]
    slot_index = jnp.arange(slot_total, dtype=jnp.int32)
    live_slots = slot_index % per_owner < counts[slot_index // per_owner]
    masked = jnp.where(live_slots[:, None, None], tiles, jnp.zeros_like(tiles))

    def advance(totals, inputs_now):
        layer_acc, grad_acc = totals
        weight_block, row_id, col_id = inputs_now
        row_at = (row_id * edge_len).astype(jnp.int32)
        col_at = (col_id * edge_len).astype(jnp.int32)
        picked = lax.dynamic_slice_in_dim(hidden, row_at, edge_len, 1)
        upstream = lax.dynamic_slice_in_dim(cotangent, col_at, edge_len, 1)
        forward = jnp.dot(picked, weight_block, preferred_element_type=jnp.float32)
        layer_acc = lax.dynamic_update_slice_in_dim(layer_acc, lax.dynamic_slice_in_dim(layer_acc, col_at, edge_len, 1) + forward, col_at, 1)
        backward = jnp.dot(upstream, weight_block.T, preferred_element_type=jnp.float32)
        grad_acc = lax.dynamic_update_slice_in_dim(grad_acc, lax.dynamic_slice_in_dim(grad_acc, row_at, edge_len, 1) + backward, row_at, 1)
        weight_term = jnp.dot(picked.T, upstream, preferred_element_type=jnp.float32)
        return ((layer_acc, grad_acc), weight_term)
    start_totals = (jnp.zeros(cotangent.shape, jnp.float32), jnp.zeros(hidden.shape, jnp.float32))
    (layer_acc, grad_acc), weight_terms = lax.scan(advance, start_totals, (masked, tile_rows, tile_cols))
    raw_grad = jnp.where(live_slots[:, None, None], weight_terms, jnp.zeros_like(weight_terms))
    squares = jnp.sum(raw_grad * raw_grad)
    entries = jnp.sum(counts).astype(jnp.float32) * edge_len * edge_len
    spread = jnp.sqrt(squares / entries)
    root_tokens = math.sqrt(TOKENS)
    factor = jnp.minimum(1.0, 0.5 * root_tokens / spread) / root_tokens
    return (layer_acc.astype(jnp.bfloat16), grad_acc.astype(jnp.bfloat16), raw_grad * factor)
```

```python
import functools
import math

import jax
import jax.numpy as jnp
from jax import lax
from jax.experimental import pallas as pl
from jax.experimental.pallas import tpu as pltpu
from jax.sharding import PartitionSpec as P

MESH = pl.DeviceIdType.MESH
F32 = jnp.float32
BF16 = jnp.bfloat16


def exchange_kernel(
    n, dp, root,
    rows_s, cols_s, cnt_s, tiles_hbm, hid_hbm, cot_hbm,
    meta_out, tiles_out, wg_out,
    hid_v, cot_v, tiles_v, meta_v, meta_s, acc, sbuf, rbuf, fin, zs, zr, za, sqz, sqf,
    in_sem, out_sem, meta_ss, meta_rs, ag_ss, ag_rs, rs_ss, rs_rs,
    zs_ss, zs_rs, za_ss, za_rs, qz_ss, qz_rs, qf_ss, qf_rs,
):
    me = lax.axis_index("fsdp")
    z = lax.axis_index("dp")
    maxb, edge = tiles_hbm.shape[0], tiles_hbm.shape[1]
    half = maxb // 2
    per = maxb // dp
    stages = n.bit_length() - 1
    chip_bits = stages - 1
    orders = [list(range(1, stages)), list(range(stages - 1, 0, -1))]
    core = lax.rem(me, 2)

    def bit_of(b):
        return lax.rem(me // (2 ** b), 2)

    def flip(value_me, b):
        return value_me + (1 - 2 * bit_of(b)) * (2 ** b)

    def fetch(source, target, sem):
        def step(i, carry):
            at = pl.ds(pl.multiple_of(i * edge, edge), edge)
            pltpu.make_async_copy(source.at[:, at], target.at[i], sem).start()
            return carry
        lax.fori_loop(0, target.shape[0], step, 0)

    own_copy = pltpu.make_async_copy(tiles_hbm, tiles_v.at[me], in_sem.at[2])
    own_copy.start()
    fetch(cot_hbm, cot_v, in_sem.at[1])
    fetch(hid_hbm, hid_v, in_sem.at[0])

    barrier = pltpu.get_barrier_semaphore()
    for k in range(1, n):
        pl.semaphore_signal(
            barrier, inc=1, device_id={"fsdp": lax.rem(me + k, n)}, device_id_type=MESH
        )
    for k in range(1, dp):
        pl.semaphore_signal(
            barrier, inc=1, device_id={"dp": lax.rem(z + k, dp)}, device_id_type=MESH
        )
    lane = lax.broadcasted_iota(jnp.int32, (8, 128), 1)
    sub = lax.broadcasted_iota(jnp.int32, (8, 128), 0)
    meta = jnp.where(sub == 2, cnt_s[0], 0)
    for j in range(maxb):
        meta = jnp.where((sub == 0) & (lane == j), rows_s[j], meta)
        meta = jnp.where((sub == 1) & (lane == j), cols_s[j], meta)
    meta_v[me] = meta
    own_copy.wait()
    pl.semaphore_wait(barrier, n - 1 + dp - 1)

    meta_copies = []
    for k in range(1, n):
        copy = pltpu.make_async_remote_copy(
            meta_v.at[me], meta_v.at[me], meta_ss.at[k - 1], meta_rs.at[k - 1],
            device_id={"fsdp": lax.rem(me + k, n)}, device_id_type=MESH,
        )
        copy.start()
        meta_copies.append(copy)

    ag_copies = {}

    def ag_send(p, i, e):
        bits = orders[p] + [0]
        owner = me
        for t in range(len(bits)):
            if (e >> t) & 1:
                owner = flip(owner, bits[t])
        piece = tiles_v.at[owner, pl.ds(p * half, half)]
        where = 2 ** i - 1 + e
        copy = pltpu.make_async_remote_copy(
            piece, piece, ag_ss.at[p, where], ag_rs.at[p, where],
            device_id={"fsdp": flip(me, bits[i])}, device_id_type=MESH,
        )
        copy.start()
        ag_copies[p, i, e] = copy

    for i in range(stages):
        for p in range(2):
            ag_send(p, i, 0)

    for copy in meta_copies:
        copy.wait_recv()
    to_smem = pltpu.make_async_copy(meta_v, meta_s, in_sem.at[3])
    to_smem.start()
    to_smem.wait()
    meta_back = pltpu.make_async_copy(meta_v, meta_out, out_sem.at[0])
    meta_back.start()
    pltpu.make_async_copy(cot_v, cot_v, in_sem.at[1]).wait()
    pltpu.make_async_copy(hid_v, hid_v, in_sem.at[0]).wait()

    def owner_at(p, e, core_bit):
        owner = core_bit
        for t, b in enumerate(orders[p]):
            ebit = lax.rem(e // (2 ** (chip_bits - 1 - t)), 2)
            owner = owner + lax.rem(bit_of(b) + 1 + ebit, 2) * (2 ** b)
        return owner

    def term(owner, j):
        return lax.dot_general(
            hid_v[meta_s[owner, 0, j]], cot_v[meta_s[owner, 1, j]],
            (((0,), (0,)), ((), ())), preferred_element_type=F32,
        )

    chips = n // 2
    offsets = [0]
    for t in range(stages):
        offsets.append(offsets[-1] + (n >> (t + 1)))

    def rs_copy(p, t, e):
        where = offsets[t] + e
        bit = 0 if t == 0 else orders[p][t - 1]
        return pltpu.make_async_remote_copy(
            sbuf.at[p, where], rbuf.at[p, where], rs_ss.at[p, where], rs_rs.at[p, where],
            device_id={"fsdp": flip(me, bit)}, device_id_type=MESH,
        )

    def foreign(e, carry):
        for p in range(2):
            owner = owner_at(p, e, 1 - core)
            for j in range(half):
                sbuf[p, e, j] = term(owner, p * half + j).astype(BF16)
            rs_copy(p, 0, e).start()
        return carry

    lax.fori_loop(0, chips, foreign, 0)

    for i in range(chip_bits):
        for p in range(2):
            for e in range(2 ** i):
                ag_copies[p, i, e].wait_recv()
                for i2 in range(i + 1, stages):
                    ag_send(p, i2, e + 2 ** i)

    def own(e, carry):
        for p in range(2):
            owner = owner_at(p, e, core)
            for j in range(half):
                acc[p, e, j] = term(owner, p * half + j)
        return carry

    lax.fori_loop(0, chips, own, 0)

    start = 0
    for t in range(stages):
        m = n >> (t + 1)
        sent = m // 2
        for e in range(m):
            for p in range(2):
                rs_copy(p, t, e).wait_recv()
                total = acc[p, start + e] + rbuf[p, offsets[t] + e].astype(F32)
                if e < sent:
                    sbuf[p, offsets[t + 1] + e] = total.astype(BF16)
                    rs_copy(p, t + 1, e).start()
                elif m > 1:
                    acc[p, start + e] = total
                else:
                    fin[pl.ds(p * half, half)] = total
                    for q in range(half // per):
                        zs[p * (half // per) + q] = total[q * per:(q + 1) * per].astype(BF16)
        start += sent

    def z_peer(r):
        return lax.rem(z + r, dp)

    z_copies = []
    for r in range(1, dp):
        copy = pltpu.make_async_remote_copy(
            zs.at[z_peer(r)], zr.at[r - 1], zs_ss.at[r - 1], zs_rs.at[r - 1],
            device_id={"dp": z_peer(r)}, device_id_type=MESH,
        )
        copy.start()
        z_copies.append(copy)

    for p in range(2):
        for e in range(2 ** chip_bits):
            ag_copies[p, chip_bits, e].wait_recv()
    tiles_back = pltpu.make_async_copy(tiles_v, tiles_out, out_sem.at[1])
    tiles_back.start()

    piece = fin[pl.ds(z * per, per)]
    for r in range(1, dp):
        z_copies[r - 1].wait_recv()
        piece = piece + zr[r - 1].astype(F32)
    slot = z * per + lax.broadcasted_iota(jnp.int32, piece.shape, 0)
    piece = piece * jnp.clip(cnt_s[0] - slot, 0, 1).astype(F32)
    za[z] = piece.astype(BF16)
    sqz[z] = jnp.sum((piece * piece).reshape(-1, 8, 128), axis=0)
    a_copies, q_copies = [], []
    for r in range(1, dp):
        copy = pltpu.make_async_remote_copy(
            sqz.at[z], sqz.at[z], qz_ss.at[r - 1], qz_rs.at[r - 1],
            device_id={"dp": z_peer(r)}, device_id_type=MESH,
        )
        copy.start()
        q_copies.append(copy)
    for r in range(1, dp):
        copy = pltpu.make_async_remote_copy(
            za.at[z], za.at[z], za_ss.at[r - 1], za_rs.at[r - 1],
            device_id={"dp": z_peer(r)}, device_id_type=MESH,
        )
        copy.start()
        a_copies.append(copy)
    for copy in q_copies:
        copy.wait_recv()
    sqf[me] = jnp.sum(sqz[...], axis=0)
    f_copies = []
    for k in range(1, n):
        copy = pltpu.make_async_remote_copy(
            sqf.at[me], sqf.at[me], qf_ss.at[k - 1], qf_rs.at[k - 1],
            device_id={"fsdp": lax.rem(me + k, n)}, device_id_type=MESH,
        )
        copy.start()
        f_copies.append(copy)
    entries = meta_s[0, 2, 0]
    for k in range(1, n):
        entries = entries + meta_s[k, 2, 0]
    for copy in a_copies + f_copies:
        copy.wait_recv()
    squares = jnp.sum(jnp.sum(sqf[...], axis=0), axis=(0, 1), keepdims=True)
    live = jnp.full((1, 1), entries, jnp.int32).astype(F32) * edge * edge
    spread = jnp.sqrt(squares / live)
    factor = jnp.minimum(1.0, 0.5 * root / spread) / root
    for q in range(dp):
        for i in range(per):
            wg_out[q * per + i] = za[q, i].astype(F32) * factor

    for copy in meta_copies + list(ag_copies.values()) + z_copies + q_copies + a_copies + f_copies:
        copy.wait_send()
    for t in range(stages):
        for e in range(n >> (t + 1)):
            for p in range(2):
                rs_copy(p, t, e).wait_send()
    meta_back.wait()
    tiles_back.wait()


def project_kernel(
    n, maxb,
    meta_s, tiles_hbm, hid_hbm, cot_hbm,
    layer_hbm, grad_hbm,
    tiles_v, cot_v, hid_v, gacc, gout, lacc, lout, zero_v,
    row_left, row_seen, col_left, col_seen,
    in_sem, hid_sem, g_sem, l_sem,
):
    edge = zero_v.shape[1]
    tile_copy = pltpu.make_async_copy(tiles_hbm, tiles_v, in_sem.at[0])
    cot_copy = pltpu.make_async_copy(cot_hbm, cot_v, in_sem.at[1])
    tile_copy.start()
    cot_copy.start()
    zero_v[...] = jnp.zeros_like(zero_v)

    def clear(left, seen):
        def step(i, carry):
            left[i] = 0
            seen[i] = 0
            return carry
        lax.fori_loop(0, left.shape[0], step, 0)

    clear(row_left, row_seen)
    clear(col_left, col_seen)

    def columns(i):
        return pl.ds(pl.multiple_of(i * edge, edge), edge)

    def each_live(visit):
        def owner(o, carry):
            def slot(j, inner):
                visit(o, j, meta_s[o, 0, j], meta_s[o, 1, j])
                return inner
            return lax.fori_loop(0, meta_s[o, 2, 0], slot, carry)
        lax.fori_loop(0, n, owner, 0)

    def fetch(o, j, row, col):
        pltpu.make_async_copy(hid_hbm.at[:, columns(row)], hid_v.at[o, j], hid_sem).start()
        row_left[row] = row_left[row] + 1
        col_left[col] = col_left[col] + 1

    each_live(fetch)

    def blank(left, target, sem):
        def step(i, carry):
            @pl.when(left[i] == 0)
            def _():
                pltpu.make_async_copy(zero_v, target.at[:, columns(i)], sem).start()
            return carry
        lax.fori_loop(0, left.shape[0], step, 0)

    blank(row_left, grad_hbm, g_sem)
    blank(col_left, layer_hbm, l_sem)
    tile_copy.wait()
    cot_copy.wait()

    def add_block(at, value, left, seen, total, out, target, sem):
        remaining = left[at] - 1
        first = seen[at] == 0
        left[at] = remaining
        seen[at] = 1

        @pl.when(first & (remaining == 0))
        def _():
            out[at] = value.astype(BF16)

        @pl.when(first & (remaining > 0))
        def _():
            total[at] = value

        @pl.when(jnp.logical_not(first) & (remaining > 0))
        def _():
            total[at] = total[at] + value

        @pl.when(jnp.logical_not(first) & (remaining == 0))
        def _():
            out[at] = (total[at] + value).astype(BF16)

        @pl.when(remaining == 0)
        def _():
            pltpu.make_async_copy(out.at[at], target.at[:, columns(at)], sem).start()

    def backward(o, j, row, col):
        value = lax.dot_general(
            cot_v[:, columns(col)], tiles_v[o, j], (((1,), (1,)), ((), ())),
            preferred_element_type=F32,
        )
        add_block(row, value, row_left, row_seen, gacc, gout, grad_hbm, g_sem)

    each_live(backward)

    def arrived(o, j, row, col):
        pltpu.make_async_copy(hid_hbm.at[:, columns(row)], hid_v.at[o, j], hid_sem).wait()

    each_live(arrived)

    def forward(o, j, row, col):
        value = jnp.dot(hid_v[o, j], tiles_v[o, j], preferred_element_type=F32)
        add_block(col, value, col_left, col_seen, lacc, lout, layer_hbm, l_sem)

    each_live(forward)
    pltpu.make_async_copy(grad_hbm, grad_hbm, g_sem).wait()
    pltpu.make_async_copy(layer_hbm, layer_hbm, l_sem).wait()


def shards(n, dp, hidden, cotangent, tiles, tile_rows, tile_cols, counts):
    tokens, width_ff = hidden.shape
    width_model = cotangent.shape[1]
    maxb, edge, _ = tiles.shape
    blocks_ff, blocks_model = width_ff // edge, width_model // edge
    root = math.sqrt(tokens * n * dp)
    half, per = maxb // 2, maxb // dp
    hbm = pl.BlockSpec(memory_space=pl.ANY)
    smem = pl.BlockSpec(memory_space=pltpu.SMEM)
    vmem = pl.BlockSpec(memory_space=pltpu.VMEM)
    dma = pltpu.SemaphoreType.DMA
    meta, gathered, weight_grad = pl.pallas_call(
        functools.partial(exchange_kernel, n, dp, root),
        out_shape=(
            jax.ShapeDtypeStruct((n, 8, 128), jnp.int32),
            jax.ShapeDtypeStruct((n, maxb, edge, edge), BF16),
            jax.ShapeDtypeStruct((maxb, edge, edge), F32),
        ),
        in_specs=[smem, smem, smem, hbm, hbm, hbm],
        out_specs=(hbm, hbm, vmem),
        scratch_shapes=[
            pltpu.VMEM((blocks_ff, tokens, edge), BF16),
            pltpu.VMEM((blocks_model, tokens, edge), BF16),
            pltpu.VMEM((n, maxb, edge, edge), BF16),
            pltpu.VMEM((n, 8, 128), jnp.int32),
            pltpu.SMEM((n, 8, 128), jnp.int32),
            pltpu.VMEM((2, n // 2, half, edge, edge), F32),
            pltpu.VMEM((2, n - 1, half, edge, edge), BF16),
            pltpu.VMEM((2, n - 1, half, edge, edge), BF16),
            pltpu.VMEM((maxb, edge, edge), F32),
            pltpu.VMEM((dp, per, edge, edge), BF16),
            pltpu.VMEM((dp - 1, per, edge, edge), BF16),
            pltpu.VMEM((dp, per, edge, edge), BF16),
            pltpu.VMEM((dp, 8, 128), F32),
            pltpu.VMEM((n, 8, 128), F32),
            dma((4,)), dma((2,)),
            dma((n - 1,)), dma((n - 1,)),
            dma((2, n - 1)), dma((2, n - 1)),
            dma((2, n - 1)), dma((2, n - 1)),
            dma((dp - 1,)), dma((dp - 1,)),
            dma((dp - 1,)), dma((dp - 1,)),
            dma((dp - 1,)), dma((dp - 1,)),
            dma((n - 1,)), dma((n - 1,)),
        ],
        compiler_params=pltpu.CompilerParams(
            collective_id=0, has_side_effects=True, vmem_limit_bytes=60 * 2 ** 20
        ),
        name="exchange",
    )(tile_rows, tile_cols, counts, tiles, hidden, cotangent)

    layer_out, hidden_grad = pl.pallas_call(
        functools.partial(project_kernel, n, maxb),
        out_shape=(
            jax.ShapeDtypeStruct(cotangent.shape, BF16),
            jax.ShapeDtypeStruct(hidden.shape, BF16),
        ),
        in_specs=[smem, hbm, hbm, hbm],
        out_specs=(hbm, hbm),
        scratch_shapes=[
            pltpu.VMEM((n, maxb, edge, edge), BF16),
            pltpu.VMEM(cotangent.shape, BF16),
            pltpu.VMEM((n, maxb, tokens, edge), BF16),
            pltpu.VMEM((blocks_ff, tokens, edge), F32),
            pltpu.VMEM((blocks_ff, tokens, edge), BF16),
            pltpu.VMEM((blocks_model, tokens, edge), F32),
            pltpu.VMEM((blocks_model, tokens, edge), BF16),
            pltpu.VMEM((tokens, edge), BF16),
            pltpu.SMEM((blocks_ff,), jnp.int32),
            pltpu.SMEM((blocks_ff,), jnp.int32),
            pltpu.SMEM((blocks_model,), jnp.int32),
            pltpu.SMEM((blocks_model,), jnp.int32),
            dma((2,)), dma, dma, dma,
        ],
        compiler_params=pltpu.CompilerParams(vmem_limit_bytes=62 * 2 ** 20),
        name="project",
    )(meta, gathered, hidden, cotangent)
    return layer_out, hidden_grad, weight_grad


def solution(mesh):
    placed = (
        P(("fsdp", "dp"), None),
        P(("fsdp", "dp"), None),
        P("fsdp", None, None),
        P("fsdp"),
        P("fsdp"),
        P("fsdp"),
    )
    return jax.shard_map(
        functools.partial(shards, mesh.shape["fsdp"], mesh.shape["dp"]),
        mesh=mesh,
        in_specs=placed,
        out_specs=(P(("fsdp", "dp"), None), P(("fsdp", "dp"), None), P("fsdp", None, None)),
        check_vma=False,
    )
```

```python
import functools
import math

import jax
import jax.numpy as jnp
from jax import lax
from jax.experimental import pallas as pl
from jax.experimental.pallas import tpu as pltpu
from jax.sharding import PartitionSpec as P

MESH = pl.DeviceIdType.MESH
F32 = jnp.float32
BF16 = jnp.bfloat16


def exchange_kernel(
    n, dp, root,
    rows_s, cols_s, cnt_s, tiles_hbm, hid_hbm, cot_hbm,
    meta_out, tiles_out, wg_out,
    hid_v, cot_v, tiles_v, meta_v, meta_s, acc, sbuf, rbuf, fin, zs, zr, za, sqz, sqf,
    in_sem, out_sem, meta_ss, meta_rs, ag_ss, ag_rs, rs_ss, rs_rs,
    zs_ss, zs_rs, za_ss, za_rs, qz_ss, qz_rs, qf_ss, qf_rs,
):
    me = lax.axis_index("fsdp")
    z = lax.axis_index("dp")
    maxb, edge = tiles_hbm.shape[0], tiles_hbm.shape[1]
    half = maxb // 2
    per = maxb // dp
    stages = n.bit_length() - 1
    chip_bits = stages - 1
    orders = [list(range(1, stages)), list(range(stages - 1, 0, -1))]
    core = lax.rem(me, 2)

    def bit_of(b):
        return lax.rem(me // (2 ** b), 2)

    def flip(value_me, b):
        return value_me + (1 - 2 * bit_of(b)) * (2 ** b)

    def fetch(source, target, sem):
        def step(i, carry):
            at = pl.ds(pl.multiple_of(i * edge, edge), edge)
            pltpu.make_async_copy(source.at[:, at], target.at[i], sem).start()
            return carry
        lax.fori_loop(0, target.shape[0], step, 0)

    own_copy = pltpu.make_async_copy(tiles_hbm, tiles_v.at[me], in_sem.at[2])
    own_copy.start()
    fetch(cot_hbm, cot_v, in_sem.at[1])
    fetch(hid_hbm, hid_v, in_sem.at[0])

    barrier = pltpu.get_barrier_semaphore()
    for k in range(1, n):
        pl.semaphore_signal(
            barrier, inc=1, device_id={"fsdp": lax.rem(me + k, n)}, device_id_type=MESH
        )
    for k in range(1, dp):
        pl.semaphore_signal(
            barrier, inc=1, device_id={"dp": lax.rem(z + k, dp)}, device_id_type=MESH
        )
    lane = lax.broadcasted_iota(jnp.int32, (8, 128), 1)
    sub = lax.broadcasted_iota(jnp.int32, (8, 128), 0)
    meta = jnp.where(sub == 2, cnt_s[0], 0)
    for j in range(maxb):
        meta = jnp.where((sub == 0) & (lane == j), rows_s[j], meta)
        meta = jnp.where((sub == 1) & (lane == j), cols_s[j], meta)
    meta_v[me] = meta
    own_copy.wait()
    pl.semaphore_wait(barrier, n - 1 + dp - 1)

    meta_copies = []
    for k in range(1, n):
        copy = pltpu.make_async_remote_copy(
            meta_v.at[me], meta_v.at[me], meta_ss.at[k - 1], meta_rs.at[k - 1],
            device_id={"fsdp": lax.rem(me + k, n)}, device_id_type=MESH,
        )
        copy.start()
        meta_copies.append(copy)

    ag_copies = {}

    def ag_send(p, i, e):
        bits = orders[p] + [0]
        owner = me
        for t in range(len(bits)):
            if (e >> t) & 1:
                owner = flip(owner, bits[t])
        piece = tiles_v.at[owner, pl.ds(p * half, half)]
        where = 2 ** i - 1 + e
        copy = pltpu.make_async_remote_copy(
            piece, piece, ag_ss.at[p, where], ag_rs.at[p, where],
            device_id={"fsdp": flip(me, bits[i])}, device_id_type=MESH,
        )
        copy.start()
        ag_copies[p, i, e] = copy

    for i in range(stages):
        for p in range(2):
            ag_send(p, i, 0)

    for copy in meta_copies:
        copy.wait_recv()
    to_smem = pltpu.make_async_copy(meta_v, meta_s, in_sem.at[3])
    to_smem.start()
    to_smem.wait()
    meta_back = pltpu.make_async_copy(meta_v, meta_out, out_sem.at[0])
    meta_back.start()
    pltpu.make_async_copy(cot_v, cot_v, in_sem.at[1]).wait()
    pltpu.make_async_copy(hid_v, hid_v, in_sem.at[0]).wait()

    def owner_at(p, e, core_bit):
        owner = core_bit
        for t, b in enumerate(orders[p]):
            ebit = lax.rem(e // (2 ** (chip_bits - 1 - t)), 2)
            owner = owner + lax.rem(bit_of(b) + 1 + ebit, 2) * (2 ** b)
        return owner

    def term(owner, j):
        return lax.dot_general(
            hid_v[meta_s[owner, 0, j]], cot_v[meta_s[owner, 1, j]],
            (((0,), (0,)), ((), ())), preferred_element_type=F32,
        )

    chips = n // 2
    offsets = [0]
    for t in range(stages):
        offsets.append(offsets[-1] + (n >> (t + 1)))

    def rs_copy(p, t, e):
        where = offsets[t] + e
        bit = 0 if t == 0 else orders[p][t - 1]
        return pltpu.make_async_remote_copy(
            sbuf.at[p, where], rbuf.at[p, where], rs_ss.at[p, where], rs_rs.at[p, where],
            device_id={"fsdp": flip(me, bit)}, device_id_type=MESH,
        )

    def foreign(e, carry):
        for p in range(2):
            owner = owner_at(p, e, 1 - core)
            for j in range(half):
                sbuf[p, e, j] = term(owner, p * half + j).astype(BF16)
            rs_copy(p, 0, e).start()
        return carry

    lax.fori_loop(0, chips, foreign, 0)

    for i in range(chip_bits):
        for p in range(2):
            for e in range(2 ** i):
                ag_copies[p, i, e].wait_recv()
                for i2 in range(i + 1, stages):
                    ag_send(p, i2, e + 2 ** i)

    def own(e, carry):
        for p in range(2):
            owner = owner_at(p, e, core)
            for j in range(half):
                acc[p, e, j] = term(owner, p * half + j)
        return carry

    lax.fori_loop(0, chips, own, 0)

    start = 0
    for t in range(stages):
        m = n >> (t + 1)
        sent = m // 2
        for e in range(m):
            for p in range(2):
                rs_copy(p, t, e).wait_recv()
                total = acc[p, start + e] + rbuf[p, offsets[t] + e].astype(F32)
                if e < sent:
                    sbuf[p, offsets[t + 1] + e] = total.astype(BF16)
                    rs_copy(p, t + 1, e).start()
                elif m > 1:
                    acc[p, start + e] = total
                else:
                    fin[pl.ds(p * half, half)] = total
                    for q in range(half // per):
                        zs[p * (half // per) + q] = total[q * per:(q + 1) * per].astype(BF16)
        start += sent

    def z_peer(r):
        return lax.rem(z + r, dp)

    z_copies = []
    for r in range(1, dp):
        copy = pltpu.make_async_remote_copy(
            zs.at[z_peer(r)], zr.at[r - 1], zs_ss.at[r - 1], zs_rs.at[r - 1],
            device_id={"dp": z_peer(r)}, device_id_type=MESH,
        )
        copy.start()
        z_copies.append(copy)

    for p in range(2):
        for e in range(2 ** chip_bits):
            ag_copies[p, chip_bits, e].wait_recv()
    tiles_back = pltpu.make_async_copy(tiles_v, tiles_out, out_sem.at[1])
    tiles_back.start()

    piece = fin[pl.ds(z * per, per)]
    for r in range(1, dp):
        z_copies[r - 1].wait_recv()
        piece = piece + zr[r - 1].astype(F32)
    slot = z * per + lax.broadcasted_iota(jnp.int32, piece.shape, 0)
    piece = piece * jnp.clip(cnt_s[0] - slot, 0, 1).astype(F32)
    za[z] = piece.astype(BF16)
    sqz[z] = jnp.sum((piece * piece).reshape(-1, 8, 128), axis=0)
    a_copies, q_copies = [], []
    for r in range(1, dp):
        copy = pltpu.make_async_remote_copy(
            sqz.at[z], sqz.at[z], qz_ss.at[r - 1], qz_rs.at[r - 1],
            device_id={"dp": z_peer(r)}, device_id_type=MESH,
        )
        copy.start()
        q_copies.append(copy)
    for r in range(1, dp):
        copy = pltpu.make_async_remote_copy(
            za.at[z], za.at[z], za_ss.at[r - 1], za_rs.at[r - 1],
            device_id={"dp": z_peer(r)}, device_id_type=MESH,
        )
        copy.start()
        a_copies.append(copy)
    for copy in q_copies:
        copy.wait_recv()
    sqf[me] = jnp.sum(sqz[...], axis=0)
    f_copies = []
    for k in range(1, n):
        copy = pltpu.make_async_remote_copy(
            sqf.at[me], sqf.at[me], qf_ss.at[k - 1], qf_rs.at[k - 1],
            device_id={"fsdp": lax.rem(me + k, n)}, device_id_type=MESH,
        )
        copy.start()
        f_copies.append(copy)
    entries = meta_s[0, 2, 0]
    for k in range(1, n):
        entries = entries + meta_s[k, 2, 0]
    for copy in a_copies + f_copies:
        copy.wait_recv()
    squares = jnp.sum(jnp.sum(sqf[...], axis=0), axis=(0, 1), keepdims=True)
    live = jnp.full((1, 1), entries, jnp.int32).astype(F32) * edge * edge
    spread = jnp.sqrt(squares / live)
    factor = jnp.minimum(1.0, 0.5 * root / spread) / root
    for q in range(dp):
        for i in range(per):
            wg_out[q * per + i] = za[q, i].astype(F32) * factor

    for copy in meta_copies + list(ag_copies.values()) + z_copies + q_copies + a_copies + f_copies:
        copy.wait_send()
    for t in range(stages):
        for e in range(n >> (t + 1)):
            for p in range(2):
                rs_copy(p, t, e).wait_send()
    meta_back.wait()
    tiles_back.wait()


def project_kernel(
    n, maxb,
    meta_s, tiles_hbm, hid_hbm, cot_hbm,
    layer_hbm, grad_hbm,
    tiles_v, cot_v, hid_v, gacc, gout, lacc, lout, zero_v, values,
    row_left, row_seen, col_left, col_seen,
    in_sem, hid_sem, g_sem, l_sem,
):
    edge = zero_v.shape[1]
    tile_copy = pltpu.make_async_copy(tiles_hbm, tiles_v, in_sem.at[0])
    cot_copy = pltpu.make_async_copy(cot_hbm, cot_v, in_sem.at[1])
    tile_copy.start()
    cot_copy.start()
    zero_v[...] = jnp.zeros_like(zero_v)

    def clear(left, seen):
        def step(i, carry):
            left[i] = 0
            seen[i] = 0
            return carry
        lax.fori_loop(0, left.shape[0], step, 0)

    clear(row_left, row_seen)
    clear(col_left, col_seen)

    def columns(i):
        return pl.ds(pl.multiple_of(i * edge, edge), edge)

    def each_live(visit):
        def owner(o, carry):
            def slot(j, inner):
                visit(o, j, meta_s[o, 0, j], meta_s[o, 1, j])
                return inner
            return lax.fori_loop(0, meta_s[o, 2, 0], slot, carry)
        lax.fori_loop(0, n, owner, 0)

    def fetch(o, j, row, col):
        pltpu.make_async_copy(hid_hbm.at[:, columns(row)], hid_v.at[o, j], hid_sem).start()
        row_left[row] = row_left[row] + 1
        col_left[col] = col_left[col] + 1

    each_live(fetch)

    def blank(left, target, sem):
        def step(i, carry):
            @pl.when(left[i] == 0)
            def _():
                pltpu.make_async_copy(zero_v, target.at[:, columns(i)], sem).start()
            return carry
        lax.fori_loop(0, left.shape[0], step, 0)

    blank(row_left, grad_hbm, g_sem)
    blank(col_left, layer_hbm, l_sem)
    tile_copy.wait()
    cot_copy.wait()

    def add_block(at, value, left, seen, total, out, target, sem):
        remaining = left[at] - 1
        first = seen[at] == 0
        left[at] = remaining
        seen[at] = 1

        @pl.when(first & (remaining == 0))
        def _():
            out[at] = value[...].astype(BF16)

        @pl.when(first & (remaining > 0))
        def _():
            total[at] = value[...]

        @pl.when(jnp.logical_not(first))
        def _():
            summed = total[at] + value[...]
            total[at] = summed
            out[at] = summed.astype(BF16)

        @pl.when(remaining == 0)
        def _():
            pltpu.make_async_copy(out.at[at], target.at[:, columns(at)], sem).start()

    def backward(o, carry):
        for j in range(maxb):
            values[j] = lax.dot_general(
                cot_v[:, columns(meta_s[o, 1, j])], tiles_v[o, j], (((1,), (1,)), ((), ())),
                preferred_element_type=F32,
            )

        def slot(j, inner):
            add_block(
                meta_s[o, 0, j], values.at[j], row_left, row_seen, gacc, gout, grad_hbm, g_sem
            )
            return inner

        return lax.fori_loop(0, meta_s[o, 2, 0], slot, carry)

    lax.fori_loop(0, n, backward, 0)

    def arrived(o, j, row, col):
        pltpu.make_async_copy(hid_hbm.at[:, columns(row)], hid_v.at[o, j], hid_sem).wait()

    each_live(arrived)

    def forward(o, carry):
        for j in range(maxb):
            values[j] = jnp.dot(hid_v[o, j], tiles_v[o, j], preferred_element_type=F32)

        def slot(j, inner):
            add_block(
                meta_s[o, 1, j], values.at[j], col_left, col_seen, lacc, lout, layer_hbm, l_sem
            )
            return inner

        return lax.fori_loop(0, meta_s[o, 2, 0], slot, carry)

    lax.fori_loop(0, n, forward, 0)
    pltpu.make_async_copy(grad_hbm, grad_hbm, g_sem).wait()
    pltpu.make_async_copy(layer_hbm, layer_hbm, l_sem).wait()


def shards(n, dp, hidden, cotangent, tiles, tile_rows, tile_cols, counts):
    tokens, width_ff = hidden.shape
    width_model = cotangent.shape[1]
    maxb, edge, _ = tiles.shape
    blocks_ff, blocks_model = width_ff // edge, width_model // edge
    root = math.sqrt(tokens * n * dp)
    half, per = maxb // 2, maxb // dp
    hbm = pl.BlockSpec(memory_space=pl.ANY)
    smem = pl.BlockSpec(memory_space=pltpu.SMEM)
    vmem = pl.BlockSpec(memory_space=pltpu.VMEM)
    dma = pltpu.SemaphoreType.DMA
    meta, gathered, weight_grad = pl.pallas_call(
        functools.partial(exchange_kernel, n, dp, root),
        out_shape=(
            jax.ShapeDtypeStruct((n, 8, 128), jnp.int32),
            jax.ShapeDtypeStruct((n, maxb, edge, edge), BF16),
            jax.ShapeDtypeStruct((maxb, edge, edge), F32),
        ),
        in_specs=[smem, smem, smem, hbm, hbm, hbm],
        out_specs=(hbm, hbm, vmem),
        scratch_shapes=[
            pltpu.VMEM((blocks_ff, tokens, edge), BF16),
            pltpu.VMEM((blocks_model, tokens, edge), BF16),
            pltpu.VMEM((n, maxb, edge, edge), BF16),
            pltpu.VMEM((n, 8, 128), jnp.int32),
            pltpu.SMEM((n, 8, 128), jnp.int32),
            pltpu.VMEM((2, n // 2, half, edge, edge), F32),
            pltpu.VMEM((2, n - 1, half, edge, edge), BF16),
            pltpu.VMEM((2, n - 1, half, edge, edge), BF16),
            pltpu.VMEM((maxb, edge, edge), F32),
            pltpu.VMEM((dp, per, edge, edge), BF16),
            pltpu.VMEM((dp - 1, per, edge, edge), BF16),
            pltpu.VMEM((dp, per, edge, edge), BF16),
            pltpu.VMEM((dp, 8, 128), F32),
            pltpu.VMEM((n, 8, 128), F32),
            dma((4,)), dma((2,)),
            dma((n - 1,)), dma((n - 1,)),
            dma((2, n - 1)), dma((2, n - 1)),
            dma((2, n - 1)), dma((2, n - 1)),
            dma((dp - 1,)), dma((dp - 1,)),
            dma((dp - 1,)), dma((dp - 1,)),
            dma((dp - 1,)), dma((dp - 1,)),
            dma((n - 1,)), dma((n - 1,)),
        ],
        compiler_params=pltpu.CompilerParams(
            collective_id=0, has_side_effects=True, vmem_limit_bytes=60 * 2 ** 20
        ),
        name="exchange",
    )(tile_rows, tile_cols, counts, tiles, hidden, cotangent)

    layer_out, hidden_grad = pl.pallas_call(
        functools.partial(project_kernel, n, maxb),
        out_shape=(
            jax.ShapeDtypeStruct(cotangent.shape, BF16),
            jax.ShapeDtypeStruct(hidden.shape, BF16),
        ),
        in_specs=[smem, hbm, hbm, hbm],
        out_specs=(hbm, hbm),
        scratch_shapes=[
            pltpu.VMEM((n, maxb, edge, edge), BF16),
            pltpu.VMEM(cotangent.shape, BF16),
            pltpu.VMEM((n, maxb, tokens, edge), BF16),
            pltpu.VMEM((blocks_ff, tokens, edge), F32),
            pltpu.VMEM((blocks_ff, tokens, edge), BF16),
            pltpu.VMEM((blocks_model, tokens, edge), F32),
            pltpu.VMEM((blocks_model, tokens, edge), BF16),
            pltpu.VMEM((tokens, edge), BF16),
            pltpu.VMEM((maxb, tokens, edge), F32),
            pltpu.SMEM((blocks_ff,), jnp.int32),
            pltpu.SMEM((blocks_ff,), jnp.int32),
            pltpu.SMEM((blocks_model,), jnp.int32),
            pltpu.SMEM((blocks_model,), jnp.int32),
            dma((2,)), dma, dma, dma,
        ],
        compiler_params=pltpu.CompilerParams(vmem_limit_bytes=62 * 2 ** 20),
        name="project",
    )(meta, gathered, hidden, cotangent)
    return layer_out, hidden_grad, weight_grad


def solution(mesh):
    placed = (
        P(("fsdp", "dp"), None),
        P(("fsdp", "dp"), None),
        P("fsdp", None, None),
        P("fsdp"),
        P("fsdp"),
        P("fsdp"),
    )
    return jax.shard_map(
        functools.partial(shards, mesh.shape["fsdp"], mesh.shape["dp"]),
        mesh=mesh,
        in_specs=placed,
        out_specs=(P(("fsdp", "dp"), None), P(("fsdp", "dp"), None), P("fsdp", None, None)),
        check_vma=False,
    )
```
